32 devices in a mesh: shot: 16 (over z, y, core), rec: 2 (over x).
Axes of the slice: x: 2, y: 2, z: 4, core: 2. Of those that a mesh axis runs over, the one named last changes fastest.
Arguments:
- survey: float32 [2, 8, 2048, 2048], P(None, None, 'shot', 'rec'), may hold values from -1.5 to 1.5
- panel_index: int32 [2], replicated, may hold values from 0 to 31
Outputs:
- predicted: float32 [64, 2048, 2048], P(None, 'shot', 'rec')
The draws below stay inside these ranges and needn't reach their ends.
Inputs may be any that keep to these rules, and one draw needn't show every extreme that they name: `panel_index`: panel numbers; one panel may come twice.
All inputs are finite; a program needn't handle non-finite values.
Results may differ from the reference program's by a relative error of at most 0.0001.
Values sent between devices are 32-bit elements; how exact they have to be, the bound alone decides.
A program may use at most 192 MiB of HBM per device.

```python
import math
import jax
import jax.numpy as jnp
from jax import lax

ORDER = 2048
FREQS = 8
FIRST_BIN = 8
TRACE_LEN = 400
SAMPLES = 64
PANEL = 64
STEPS = 2


def steps_of(own_key, extent, split, least, high):
    level = 1.0
    for axis_at, shards_of in split:
        heights = jax.random.uniform(jax.random.fold_in(jax.random.fold_in(own_key, 6), axis_at), (shards_of,), jnp.float32, least / len(split), high / len(split))
        level = level * jnp.repeat(jnp.exp(heights), extent[axis_at] // shards_of).reshape((-1,) + (1,) * (len(extent) - 1 - axis_at))
    return level


def gaussian(own_key, extent, width, limit, split=(), kind=jnp.bfloat16):
    loudness = steps_of(own_key, extent, split, -0.22, 0.18) if split else 1.0
    entries = jax.random.normal(own_key, extent, jnp.float32) * width * loudness
    return jnp.minimum(jnp.maximum(entries, -limit), limit).astype(kind)


def setup_inputs(seed: int = 0) -> dict:
    arg_keys = jax.random.split(jax.random.key(seed), 3)
    survey = gaussian(arg_keys[0], (2, FREQS, ORDER, ORDER), 0.25, 1.5, ((2, 16), (3, 2)), jnp.float32)
    panel_index = jax.random.randint(arg_keys[1], (STEPS,), 0, ORDER // PANEL).astype(jnp.int32)
    return dict(survey=survey, panel_index=panel_index)


def build_tables(nfreq):
    bins = jnp.arange(nfreq, dtype=jnp.int32) + FIRST_BIN
    moments = jnp.arange(SAMPLES, dtype=jnp.int32)
    phase = moments[:, None] * bins[None, :] % TRACE_LEN
    angle = phase.astype(jnp.float32) * (2.0 * math.pi / TRACE_LEN)
    factor = 1.0 / math.sqrt(nfreq)
    return (jnp.cos(angle) * factor, jnp.sin(angle) * factor)

def multiply(left_operand, right_operand):
    return jnp.einsum('vdb,vbg->vdg', left_operand, right_operand, precision=lax.Precision.HIGHEST, preferred_element_type=jnp.float32)

def reference(survey, panel_index):
    real_part = survey[0]
    imag_part = survey[1]
    cosine_lookup, sine_lookup = build_tables(FREQS)
    height = min(ORDER, 256)
    outputs = []
    for block_start in range(0, ORDER, height):
        running_real = jnp.zeros((FREQS, height, ORDER), jnp.float32)
        running_imaginary = jnp.zeros((FREQS, height, ORDER), jnp.float32)
        for index_step in range(STEPS):
            start = (panel_index[index_step] * PANEL).astype(jnp.int32)
            left_real = lax.dynamic_slice_in_dim(real_part[:, block_start:block_start + height], start, PANEL, 2)
            left_imag = lax.dynamic_slice_in_dim(imag_part[:, block_start:block_start + height], start, PANEL, 2)
            right_real = lax.dynamic_slice_in_dim(real_part, start, PANEL, 1)
            right_imag = lax.dynamic_slice_in_dim(imag_part, start, PANEL, 1)
            running_real = running_real + (multiply(left_real, right_real) - multiply(left_imag, right_imag))
            running_imaginary = running_imaginary + (multiply(left_real, right_imag) + multiply(left_imag, right_real))
        time_domain_output = jnp.einsum('ay,yjk->ajk', cosine_lookup, running_real, precision=lax.Precision.HIGHEST, preferred_element_type=jnp.float32)
        time_domain_output = time_domain_output - jnp.einsum('ay,yjk->ajk', sine_lookup, running_imaginary, precision=lax.Precision.HIGHEST, preferred_element_type=jnp.float32)
        outputs.append(time_domain_output)
    return jnp.concatenate(outputs, axis=1)
```

```python
import functools
import math

import jax
import jax.numpy as jnp
import numpy as np
from jax import lax
from jax.experimental import pallas as pl
from jax.experimental.pallas import tpu as pltpu
from jax.sharding import PartitionSpec as P

FIRST_BIN = 8
TRACE_LEN = 400
SAMPLES = 64
PANEL = 64
STEPS = 2
PIECE_ROWS = 32


def from_root(array, axis, root):
    mine = lax.axis_index(axis) == root
    return lax.psum(jnp.where(mine, array, jnp.zeros_like(array)), axis)


def table(nfreq):
    bins = np.arange(nfreq) + FIRST_BIN
    moments = np.arange(SAMPLES)
    angle = (moments[:, None] * bins[None, :] % TRACE_LEN) * (2.0 * math.pi / TRACE_LEN)
    both = np.concatenate([np.cos(angle), -np.sin(angle)], axis=1)
    return (both / math.sqrt(nfreq)).astype(np.float32)


def kron_table(nfreq):
    flat = np.kron(table(nfreq), np.eye(8, dtype=np.float32))
    hi = flat.astype(jnp.bfloat16)
    lo = (flat - hi.astype(np.float32)).astype(jnp.bfloat16)
    return np.concatenate([hi, hi, lo], axis=1)


def broadcast_kernel(owner, depth, x_ref, o_ref, send_sem, recv_sem, local_sem):
    me = lax.axis_index("shot")
    z, y, c = me // 4, (me // 2) % 2, me % 2
    z0, y0, c0 = owner // 4, (owner // 2) % 2, owner % 2
    back = z0 + 1 if z0 < depth - 1 else z0 - 1
    count = x_ref.shape[1]
    prim = c == c0
    is_owner = me == owner
    peer = me + 1 - 2 * c

    def edges(h):
        yh = y0 if h == 0 else 1 - y0
        up = prim & (y == yh) & (z >= z0) & (z < depth - 1)
        down = prim & (y == yh) & (z <= z0) & (z > 0)
        if h == 0:
            extra = prim & (y == 1 - y0) & (z == back)
            if back > z0:
                down = down | extra
            else:
                up = up | extra
            cross = prim & (y == y0) & (z != z0)
        else:
            cross = prim & (((y == 1 - y0) & (z != z0)) | is_owner)
        return [
            (0, up, me + 4),
            (1, down, me - 4),
            (2, cross, me + 2 - 4 * y),
            (3, prim, peer),
        ]

    def copy(src, h, k, slot, target):
        return pltpu.make_async_remote_copy(
            src_ref=src.at[h, k],
            dst_ref=o_ref.at[h, k],
            send_sem=send_sem.at[h, slot, k],
            recv_sem=recv_sem.at[h, k],
            device_id={"shot": target},
            device_id_type=pl.DeviceIdType.MESH,
        )

    local = pltpu.make_async_copy(x_ref, o_ref, local_sem)

    @pl.when(is_owner)
    def _():
        def step(k, carry):
            for h in (0, 1):
                for slot, cond, target in edges(h):
                    @pl.when(cond)
                    def _():
                        copy(x_ref, h, k, slot, target).start()
            return carry

        lax.fori_loop(0, count, step, 0)
        local.start()
        local.wait()

    @pl.when(jnp.logical_not(is_owner))
    def _():
        def step(k, carry):
            for h in (0, 1):
                copy(o_ref, h, k, 3, peer).wait_recv()
                for slot, cond, target in edges(h):
                    @pl.when(cond)
                    def _():
                        copy(o_ref, h, k, slot, target).start()
            return carry

        lax.fori_loop(0, count, step, 0)

    def finish(k, carry):
        for h in (0, 1):
            for slot, cond, target in edges(h):
                @pl.when(cond)
                def _():
                    copy(o_ref, h, k, slot, target).wait_send()
        return carry

    lax.fori_loop(0, count, finish, 0)


def broadcast_rows(piece, owner, shots):
    shape = piece.shape
    count = shape[1] * shape[2] // PIECE_ROWS
    flat = piece.reshape(2, count, PIECE_ROWS, shape[3])

    def call(device):
        return pl.pallas_call(
            functools.partial(broadcast_kernel, device, shots // 4),
            out_shape=jax.ShapeDtypeStruct(flat.shape, flat.dtype),
            in_specs=[pl.BlockSpec(memory_space=pl.ANY)],
            out_specs=pl.BlockSpec(memory_space=pl.ANY),
            scratch_shapes=[
                pltpu.SemaphoreType.DMA((2, 4, count)),
                pltpu.SemaphoreType.DMA((2, count)),
                pltpu.SemaphoreType.DMA,
            ],
            compiler_params=pltpu.CompilerParams(has_side_effects=True),
            name="rows_from_%d" % device,
        )

    out = lax.switch(owner, [call(device) for device in range(shots)], flat)
    return out.reshape(shape)


def split(array):
    hi = array.astype(jnp.bfloat16)
    return hi, (array - hi.astype(jnp.float32)).astype(jnp.bfloat16)


def dot(left, right):
    return jnp.dot(left, right, preferred_element_type=jnp.float32)


def predict_kernel(
    own_ref, mine_ref, other_ref, row0_ref, row1_ref, table_ref, out_ref,
    left_hi, left_lo, freq_ref,
):
    nfreq = mine_ref.shape[1]
    rows = mine_ref.shape[2]
    tile = out_ref.shape[2]

    @pl.when(pl.program_id(0) == 0)
    def _():
        lane = lax.broadcasted_iota(jnp.int32, (rows, 2 * PANEL), 1)
        own = jnp.where(lane < PANEL, own_ref[0], own_ref[1]) == 1
        for f in range(nfreq):
            real = jnp.where(own, mine_ref[0, f], other_ref[0, f])
            imag = jnp.where(own, mine_ref[1, f], other_ref[1, f])
            top = jnp.concatenate([real, -imag], axis=1)
            low = jnp.concatenate([imag, real], axis=1)
            hi, lo = split(jnp.concatenate([top, low], axis=0))
            left_hi[f] = hi
            left_lo[f] = lo

    for f in range(nfreq):
        right = jnp.concatenate(
            [row0_ref[0, f], row1_ref[0, f], row0_ref[1, f], row1_ref[1, f]], axis=0
        )
        hi, lo = split(right)
        both = dot(left_hi[f], hi) + dot(left_lo[f], hi) + dot(left_hi[f], lo)
        freq_ref[f] = both[:rows]
        freq_ref[nfreq + f] = both[rows:]

    for g in range(rows // 8):
        part = freq_ref[:, 8 * g : 8 * g + 8, :].reshape(16 * nfreq, tile)
        hi, lo = split(part)
        done = dot(table_ref[...], jnp.concatenate([hi, lo, hi], axis=0))
        out_ref[:, 8 * g : 8 * g + 8, :] = done.reshape(SAMPLES, 8, tile)


def predict(own, mine, other, row0, row1):
    _, nfreq, rows, width = mine.shape
    cols = row0.shape[3]
    tile = min(256, cols)
    big = jnp.asarray(kron_table(nfreq))
    whole = pl.BlockSpec(mine.shape, lambda j: (0, 0, 0, 0))
    row_spec = pl.BlockSpec((2, nfreq, PANEL, tile), lambda j: (0, 0, 0, j))
    return pl.pallas_call(
        predict_kernel,
        grid=(cols // tile,),
        out_shape=jax.ShapeDtypeStruct((SAMPLES, rows, cols), jnp.float32),
        in_specs=[
            pl.BlockSpec(memory_space=pltpu.SMEM),
            whole,
            whole,
            row_spec,
            row_spec,
            pl.BlockSpec(big.shape, lambda j: (0, 0)),
        ],
        out_specs=pl.BlockSpec((SAMPLES, rows, tile), lambda j: (0, 0, j)),
        scratch_shapes=[
            pltpu.VMEM((nfreq, 2 * rows, 4 * PANEL), jnp.bfloat16),
            pltpu.VMEM((nfreq, 2 * rows, 4 * PANEL), jnp.bfloat16),
            pltpu.VMEM((2 * nfreq, rows, tile), jnp.float32),
        ],
        compiler_params=pltpu.CompilerParams(vmem_limit_bytes=48 << 20),
        name="predict",
    )(own, mine, other, row0, row1, big)


def fetch_rows(source, start, shot_rows):
    length = min(shot_rows, PANEL)
    pieces = []
    for index_piece in range(PANEL // length):
        first = start + index_piece * length
        owner = first // shot_rows
        offset = first % shot_rows
        piece = lax.dynamic_slice_in_dim(source, offset, length, 2)
        pieces.append(from_root(piece, "shot", owner))
    return jnp.concatenate(pieces, axis=2)


def shards(tree, shots, recs, survey, panel_index):
    shot_rows = survey.shape[2]
    rec_cols = survey.shape[3]
    starts = [panel_index[step] * PANEL for step in range(STEPS)]
    columns = [
        lax.dynamic_slice_in_dim(survey, start % rec_cols, PANEL, 3) for start in starts
    ]
    owners = jnp.stack([start // rec_cols for start in starts])
    me = lax.axis_index("rec")
    mine = jnp.concatenate(columns, axis=3)
    if tree:
        other = lax.ppermute(mine, "rec", [(0, 1), (1, 0)])
        own = (owners == me).astype(jnp.int32)
        rows = []
        for start in starts:
            piece = lax.dynamic_slice_in_dim(survey, start % shot_rows, PANEL, 2)
            rows.append(broadcast_rows(piece, start // shot_rows, shots))
    else:
        wanted = jnp.repeat(owners == me, PANEL, total_repeat_length=STEPS * PANEL)
        mine = lax.psum(jnp.where(wanted, mine, 0.0), "rec")
        other = mine
        own = jnp.ones((STEPS,), jnp.int32)
        rows = [fetch_rows(survey, start, shot_rows) for start in starts]
    return predict(own, mine, other, rows[0], rows[1])


def solution(mesh):
    shots, recs = mesh.shape["shot"], mesh.shape["rec"]
    tree = (shots, recs) == (16, 2)
    return jax.shard_map(
        functools.partial(shards, tree, shots, recs),
        mesh=mesh,
        in_specs=(P(None, None, "shot", "rec"), P()),
        out_specs=P(None, "shot", "rec"),
        check_vma=False,
    )
```

```python
import functools
import math

import jax
import jax.numpy as jnp
import numpy as np
from jax import lax
from jax.experimental import pallas as pl
from jax.experimental.pallas import tpu as pltpu
from jax.sharding import PartitionSpec as P

FIRST_BIN = 8
TRACE_LEN = 400
SAMPLES = 64
PANEL = 64
STEPS = 2
PIECE_ROWS = 32


def from_root(array, axis, root):
    mine = lax.axis_index(axis) == root
    return lax.psum(jnp.where(mine, array, jnp.zeros_like(array)), axis)


def table(nfreq):
    bins = np.arange(nfreq) + FIRST_BIN
    moments = np.arange(SAMPLES)
    angle = (moments[:, None] * bins[None, :] % TRACE_LEN) * (2.0 * math.pi / TRACE_LEN)
    both = np.concatenate([np.cos(angle), -np.sin(angle)], axis=1)
    return (both / math.sqrt(nfreq)).astype(np.float32)


def kron_table(nfreq):
    flat = np.kron(table(nfreq), np.eye(8, dtype=np.float32))
    hi = flat.astype(jnp.bfloat16)
    lo = (flat - hi.astype(np.float32)).astype(jnp.bfloat16)
    return np.concatenate([hi, hi, lo], axis=1)


def broadcast_kernel(owner, depth, x_ref, o_ref, send_sem, recv_sem):
    del x_ref
    me = lax.axis_index("shot")
    z, y, c = me // 4, (me // 2) % 2, me % 2
    z0, y0, c0 = owner // 4, (owner // 2) % 2, owner % 2
    back = z0 + 1 if z0 < depth - 1 else z0 - 1
    count = o_ref.shape[1]
    is_owner = me == owner
    half = (c + c0) % 2
    main = (y + y0 + half) % 2 == 0
    root = (half == 1) & (z == z0) & (y == y0)
    extra = (half == 0) & (z == back) & (y != y0)
    up = main & (z >= z0) & (z < depth - 1)
    down = main & (z <= z0) & (z > 0)
    if back > z0:
        down = down | extra
    else:
        up = up | extra
    peer = me + 1 - 2 * c
    edges = [
        (0, up, me + 4),
        (1, down, me - 4),
        (2, (main & (z != z0)) | root, me + 2 - 4 * y),
        (3, jnp.logical_not(root), peer),
    ]

    def copy(h, k, slot, target):
        return pltpu.make_async_remote_copy(
            src_ref=o_ref.at[h, k],
            dst_ref=o_ref.at[h, k],
            send_sem=send_sem.at[h, slot, k],
            recv_sem=recv_sem.at[h, k],
            device_id={"shot": target},
            device_id_type=pl.DeviceIdType.MESH,
        )

    def forward(k):
        for slot, cond, target in edges:
            @pl.when(cond)
            def _():
                copy(half, k, slot, target).start()

    def loop(body):
        def step(k, carry):
            body(k)
            return carry

        lax.fori_loop(0, count, step, 0)

    @pl.when(is_owner)
    def _():
        def step(k):
            copy(1, k, 3, peer).start()
            forward(k)

        loop(step)
        loop(lambda k: copy(1, k, 3, peer).wait_send())

    @pl.when(jnp.logical_not(is_owner))
    def _():
        def step(k):
            copy(half, k, 3, peer).wait_recv()
            forward(k)

        loop(step)
        loop(lambda k: copy(1 - half, k, 3, peer).wait_recv())

    def finish(k):
        for slot, cond, target in edges:
            @pl.when(cond)
            def _():
                copy(half, k, slot, target).wait_send()

    loop(finish)


def broadcast_rows(piece, owner, shots):
    shape = piece.shape
    count = shape[1] * shape[2] // PIECE_ROWS
    flat = piece.reshape(2, count, PIECE_ROWS, shape[3])

    def call(device):
        return pl.pallas_call(
            functools.partial(broadcast_kernel, device, shots // 4),
            out_shape=jax.ShapeDtypeStruct(flat.shape, flat.dtype),
            in_specs=[pl.BlockSpec(memory_space=pl.ANY)],
            out_specs=pl.BlockSpec(memory_space=pl.ANY),
            scratch_shapes=[
                pltpu.SemaphoreType.DMA((2, 4, count)),
                pltpu.SemaphoreType.DMA((2, count)),
            ],
            input_output_aliases={0: 0},
            compiler_params=pltpu.CompilerParams(has_side_effects=True),
            name="rows_from_%d" % device,
        )

    out = lax.switch(owner, [call(device) for device in range(shots)], flat)
    return out.reshape(shape)


def split(array):
    hi = array.astype(jnp.bfloat16)
    return hi, (array - hi.astype(jnp.float32)).astype(jnp.bfloat16)


def dot(left, right):
    return jnp.dot(left, right, preferred_element_type=jnp.float32)


def predict_kernel(
    own_ref, mine_ref, other_ref, row0_ref, row1_ref, table_ref, out_ref,
    left_hi, left_lo, freq_ref,
):
    nfreq = mine_ref.shape[1]
    rows = mine_ref.shape[2]
    tile = out_ref.shape[2]

    @pl.when(pl.program_id(0) == 0)
    def _():
        lane = lax.broadcasted_iota(jnp.int32, (rows, 2 * PANEL), 1)
        own = jnp.where(lane < PANEL, own_ref[0], own_ref[1]) == 1
        for f in range(nfreq):
            real = jnp.where(own, mine_ref[0, f], other_ref[0, f])
            imag = jnp.where(own, mine_ref[1, f], other_ref[1, f])
            top = jnp.concatenate([real, -imag], axis=1)
            low = jnp.concatenate([imag, real], axis=1)
            hi, lo = split(jnp.concatenate([top, low], axis=0))
            left_hi[f] = hi
            left_lo[f] = lo

    for f in range(nfreq):
        right = jnp.concatenate(
            [row0_ref[0, f], row1_ref[0, f], row0_ref[1, f], row1_ref[1, f]], axis=0
        )
        hi, lo = split(right)
        both = dot(left_hi[f], hi) + dot(left_lo[f], hi) + dot(left_hi[f], lo)
        freq_ref[f] = both[:rows]
        freq_ref[nfreq + f] = both[rows:]

    for g in range(rows // 8):
        part = freq_ref[:, 8 * g : 8 * g + 8, :].reshape(16 * nfreq, tile)
        hi, lo = split(part)
        done = dot(table_ref[...], jnp.concatenate([hi, lo, hi], axis=0))
        out_ref[:, 8 * g : 8 * g + 8, :] = done.reshape(SAMPLES, 8, tile)


def predict(own, mine, other, row0, row1):
    _, nfreq, rows, width = mine.shape
    cols = row0.shape[3]
    tile = min(256, cols)
    big = jnp.asarray(kron_table(nfreq))
    whole = pl.BlockSpec(mine.shape, lambda j: (0, 0, 0, 0))
    row_spec = pl.BlockSpec((2, nfreq, PANEL, tile), lambda j: (0, 0, 0, j))
    return pl.pallas_call(
        predict_kernel,
        grid=(cols // tile,),
        out_shape=jax.ShapeDtypeStruct((SAMPLES, rows, cols), jnp.float32),
        in_specs=[
            pl.BlockSpec(memory_space=pltpu.SMEM),
            whole,
            whole,
            row_spec,
            row_spec,
            pl.BlockSpec(big.shape, lambda j: (0, 0)),
        ],
        out_specs=pl.BlockSpec((SAMPLES, rows, tile), lambda j: (0, 0, j)),
        scratch_shapes=[
            pltpu.VMEM((nfreq, 2 * rows, 4 * PANEL), jnp.bfloat16),
            pltpu.VMEM((nfreq, 2 * rows, 4 * PANEL), jnp.bfloat16),
            pltpu.VMEM((2 * nfreq, rows, tile), jnp.float32),
        ],
        compiler_params=pltpu.CompilerParams(vmem_limit_bytes=48 << 20),
        name="predict",
    )(own, mine, other, row0, row1, big)


def fetch_rows(source, start, shot_rows):
    length = min(shot_rows, PANEL)
    pieces = []
    for index_piece in range(PANEL // length):
        first = start + index_piece * length
        owner = first // shot_rows
        offset = first % shot_rows
        piece = lax.dynamic_slice_in_dim(source, offset, length, 2)
        pieces.append(from_root(piece, "shot", owner))
    return jnp.concatenate(pieces, axis=2)


def shards(tree, shots, recs, survey, panel_index):
    shot_rows = survey.shape[2]
    rec_cols = survey.shape[3]
    starts = [panel_index[step] * PANEL for step in range(STEPS)]
    columns = [
        lax.dynamic_slice_in_dim(survey, start % rec_cols, PANEL, 3) for start in starts
    ]
    owners = jnp.stack([start // rec_cols for start in starts])
    me = lax.axis_index("rec")
    mine = jnp.concatenate(columns, axis=3)
    if tree:
        other = lax.ppermute(mine, "rec", [(0, 1), (1, 0)])
        own = (owners == me).astype(jnp.int32)
        rows = []
        for start in starts:
            piece = lax.dynamic_slice_in_dim(survey, start % shot_rows, PANEL, 2)
            rows.append(broadcast_rows(piece, start // shot_rows, shots))
    else:
        wanted = jnp.repeat(owners == me, PANEL, total_repeat_length=STEPS * PANEL)
        mine = lax.psum(jnp.where(wanted, mine, 0.0), "rec")
        other = mine
        own = jnp.ones((STEPS,), jnp.int32)
        rows = [fetch_rows(survey, start, shot_rows) for start in starts]
    return predict(own, mine, other, rows[0], rows[1])


def solution(mesh):
    shots, recs = mesh.shape["shot"], mesh.shape["rec"]
    tree = (shots, recs) == (16, 2)
    return jax.shard_map(
        functools.partial(shards, tree, shots, recs),
        mesh=mesh,
        in_specs=(P(None, None, "shot", "rec"), P()),
        out_specs=P(None, "shot", "rec"),
        check_vma=False,
    )
```

```python
import functools
import math

import jax
import jax.numpy as jnp
import numpy as np
from jax import lax
from jax.experimental import pallas as pl
from jax.experimental.pallas import tpu as pltpu
from jax.sharding import PartitionSpec as P

FIRST_BIN = 8
TRACE_LEN = 400
SAMPLES = 64
PANEL = 64
STEPS = 2
PIECE_ROWS = 16


def from_root(array, axis, root):
    mine = lax.axis_index(axis) == root
    return lax.psum(jnp.where(mine, array, jnp.zeros_like(array)), axis)


def table(nfreq):
    bins = np.arange(nfreq) + FIRST_BIN
    moments = np.arange(SAMPLES)
    angle = (moments[:, None] * bins[None, :] % TRACE_LEN) * (2.0 * math.pi / TRACE_LEN)
    both = np.concatenate([np.cos(angle), -np.sin(angle)], axis=1)
    return (both / math.sqrt(nfreq)).astype(np.float32)


def kron_table(nfreq):
    flat = np.kron(table(nfreq), np.eye(8, dtype=np.float32))
    hi = flat.astype(jnp.bfloat16)
    lo = (flat - hi.astype(np.float32)).astype(jnp.bfloat16)
    return np.concatenate([hi, hi, lo], axis=1)


def broadcast_kernel(owner, depth, x_ref, o_ref, send_sem, recv_sem, whole_sem):
    del x_ref
    me = lax.axis_index("shot")
    z, y, c = me // 4, (me // 2) % 2, me % 2
    z0, y0, c0 = owner // 4, (owner // 2) % 2, owner % 2
    back = z0 + 1 if z0 < depth - 1 else z0 - 1
    count = o_ref.shape[1]
    is_owner = me == owner
    half = (c + c0) % 2
    main = (y + y0 + half) % 2 == 0
    root = (half == 1) & (z == z0) & (y == y0)
    extra = (half == 0) & (z == back) & (y != y0)
    up = main & (z >= z0) & (z < depth - 1)
    down = main & (z <= z0) & (z > 0)
    if back > z0:
        down = down | extra
    else:
        up = up | extra
    peer = me + 1 - 2 * c
    edges = [
        (0, up, me + 4),
        (1, down, me - 4),
        (2, (main & (z != z0)) | root, me + 2 - 4 * y),
        (3, jnp.logical_not(root), peer),
    ]

    def copy(at, send, arrive, target):
        return pltpu.make_async_remote_copy(
            src_ref=o_ref.at[at],
            dst_ref=o_ref.at[at],
            send_sem=send_sem.at[send],
            recv_sem=arrive,
            device_id={"shot": target},
            device_id_type=pl.DeviceIdType.MESH,
        )

    def forward(k):
        for slot, cond, target in edges:
            @pl.when(cond)
            def _():
                arrive = whole_sem if slot == 3 else recv_sem.at[k]
                copy((half, k), slot, arrive, target).start()

    def loop(body):
        def step(k, carry):
            body(k)
            return carry

        lax.fori_loop(0, count, step, 0)

    @pl.when(is_owner)
    def _():
        def step(k):
            copy((1, k), 4, recv_sem.at[k], peer).start()
            forward(k)

        loop(step)
        copy(1, 4, whole_sem, peer).wait_send()

    @pl.when(jnp.logical_not(is_owner))
    def _():
        def step(k):
            copy((half, k), 3, recv_sem.at[k], peer).wait_recv()
            forward(k)

        loop(step)
        copy(1 - half, 3, whole_sem, peer).wait_recv()

    for slot, cond, target in edges:
        @pl.when(cond)
        def _():
            copy(half, slot, whole_sem, target).wait_send()


def broadcast_rows(piece, owner, shots):
    shape = piece.shape
    count = shape[1] * shape[2] // PIECE_ROWS
    flat = piece.reshape(2, count, PIECE_ROWS, shape[3])

    def call(device):
        return pl.pallas_call(
            functools.partial(broadcast_kernel, device, shots // 4),
            out_shape=jax.ShapeDtypeStruct(flat.shape, flat.dtype),
            in_specs=[pl.BlockSpec(memory_space=pl.ANY)],
            out_specs=pl.BlockSpec(memory_space=pl.ANY),
            scratch_shapes=[
                pltpu.SemaphoreType.DMA((5,)),
                pltpu.SemaphoreType.DMA((count,)),
                pltpu.SemaphoreType.DMA,
            ],
            input_output_aliases={0: 0},
            compiler_params=pltpu.CompilerParams(has_side_effects=True),
            name="rows_from_%d" % device,
        )

    out = lax.switch(owner, [call(device) for device in range(shots)], flat)
    return out.reshape(shape)


def split(array):
    hi = array.astype(jnp.bfloat16)
    return hi, (array - hi.astype(jnp.float32)).astype(jnp.bfloat16)


def dot(left, right):
    return jnp.dot(left, right, preferred_element_type=jnp.float32)


def predict_kernel(
    own_ref, mine_ref, other_ref, row0_ref, row1_ref, table_ref, out_ref,
    left_hi, left_lo, freq_ref,
):
    nfreq = mine_ref.shape[1]
    rows = mine_ref.shape[2]
    tile = out_ref.shape[2]

    @pl.when(pl.program_id(0) == 0)
    def _():
        lane = lax.broadcasted_iota(jnp.int32, (rows, 2 * PANEL), 1)
        own = jnp.where(lane < PANEL, own_ref[0], own_ref[1]) == 1
        for f in range(nfreq):
            real = jnp.where(own, mine_ref[0, f], other_ref[0, f])
            imag = jnp.where(own, mine_ref[1, f], other_ref[1, f])
            top = jnp.concatenate([real, -imag], axis=1)
            low = jnp.concatenate([imag, real], axis=1)
            hi, lo = split(jnp.concatenate([top, low], axis=0))
            left_hi[f] = hi
            left_lo[f] = lo

    for f in range(nfreq):
        right = jnp.concatenate(
            [row0_ref[0, f], row1_ref[0, f], row0_ref[1, f], row1_ref[1, f]], axis=0
        )
        hi, lo = split(right)
        both = dot(left_hi[f], hi) + dot(left_lo[f], hi) + dot(left_hi[f], lo)
        freq_ref[f] = both[:rows]
        freq_ref[nfreq + f] = both[rows:]

    for g in range(rows // 8):
        part = freq_ref[:, 8 * g : 8 * g + 8, :].reshape(16 * nfreq, tile)
        hi, lo = split(part)
        done = dot(table_ref[...], jnp.concatenate([hi, lo, hi], axis=0))
        out_ref[:, 8 * g : 8 * g + 8, :] = done.reshape(SAMPLES, 8, tile)


def predict(own, mine, other, row0, row1):
    _, nfreq, rows, width = mine.shape
    cols = row0.shape[3]
    tile = min(256, cols)
    big = jnp.asarray(kron_table(nfreq))
    whole = pl.BlockSpec(mine.shape, lambda j: (0, 0, 0, 0))
    row_spec = pl.BlockSpec((2, nfreq, PANEL, tile), lambda j: (0, 0, 0, j))
    return pl.pallas_call(
        predict_kernel,
        grid=(cols // tile,),
        out_shape=jax.ShapeDtypeStruct((SAMPLES, rows, cols), jnp.float32),
        in_specs=[
            pl.BlockSpec(memory_space=pltpu.SMEM),
            whole,
            whole,
            row_spec,
            row_spec,
            pl.BlockSpec(big.shape, lambda j: (0, 0)),
        ],
        out_specs=pl.BlockSpec((SAMPLES, rows, tile), lambda j: (0, 0, j)),
        scratch_shapes=[
            pltpu.VMEM((nfreq, 2 * rows, 4 * PANEL), jnp.bfloat16),
            pltpu.VMEM((nfreq, 2 * rows, 4 * PANEL), jnp.bfloat16),
            pltpu.VMEM((2 * nfreq, rows, tile), jnp.float32),
        ],
        compiler_params=pltpu.CompilerParams(vmem_limit_bytes=48 << 20),
        name="predict",
    )(own, mine, other, row0, row1, big)


def fetch_rows(source, start, shot_rows):
    length = min(shot_rows, PANEL)
    pieces = []
    for index_piece in range(PANEL // length):
        first = start + index_piece * length
        owner = first // shot_rows
        offset = first % shot_rows
        piece = lax.dynamic_slice_in_dim(source, offset, length, 2)
        pieces.append(from_root(piece, "shot", owner))
    return jnp.concatenate(pieces, axis=2)


def shards(tree, shots, recs, survey, panel_index):
    shot_rows = survey.shape[2]
    rec_cols = survey.shape[3]
    starts = [panel_index[step] * PANEL for step in range(STEPS)]
    columns = [
        lax.dynamic_slice_in_dim(survey, start % rec_cols, PANEL, 3) for start in starts
    ]
    owners = jnp.stack([start // rec_cols for start in starts])
    me = lax.axis_index("rec")
    mine = jnp.concatenate(columns, axis=3)
    if tree:
        other = lax.ppermute(mine, "rec", [(0, 1), (1, 0)])
        own = (owners == me).astype(jnp.int32)
        rows = []
        for start in starts:
            piece = lax.dynamic_slice_in_dim(survey, start % shot_rows, PANEL, 2)
            rows.append(broadcast_rows(piece, start // shot_rows, shots))
    else:
        wanted = jnp.repeat(owners == me, PANEL, total_repeat_length=STEPS * PANEL)
        mine = lax.psum(jnp.where(wanted, mine, 0.0), "rec")
        other = mine
        own = jnp.ones((STEPS,), jnp.int32)
        rows = [fetch_rows(survey, start, shot_rows) for start in starts]
    return predict(own, mine, other, rows[0], rows[1])


def solution(mesh):
    shots, recs = mesh.shape["shot"], mesh.shape["rec"]
    tree = (shots, recs) == (16, 2)
    return jax.shard_map(
        functools.partial(shards, tree, shots, recs),
        mesh=mesh,
        in_specs=(P(None, None, "shot", "rec"), P()),
        out_specs=P(None, "shot", "rec"),
        check_vma=False,
    )
```

```python
import functools
import math

import jax
import jax.numpy as jnp
import numpy as np
from jax import lax
from jax.experimental import pallas as pl
from jax.experimental.pallas import tpu as pltpu
from jax.sharding import PartitionSpec as P

FIRST_BIN = 8
TRACE_LEN = 400
SAMPLES = 64
PANEL = 64
STEPS = 2
PIECE_ROWS = 16


def from_root(array, axis, root):
    mine = lax.axis_index(axis) == root
    return lax.psum(jnp.where(mine, array, jnp.zeros_like(array)), axis)


def middle(f):
    angle = 2.0 * math.pi * (f + FIRST_BIN) * (0.5 * (SAMPLES - 1)) / TRACE_LEN
    return math.cos(angle), math.sin(angle)


def kron_tables(nfreq):
    moments = np.arange(SAMPLES // 2) + 0.5
    bins = np.arange(nfreq) + FIRST_BIN
    angle = moments[:, None] * bins[None, :] * (2.0 * math.pi / TRACE_LEN)
    parts = []
    for wave in (np.cos(angle), np.sin(angle)):
        flat = np.kron(wave / math.sqrt(nfreq), np.eye(8)).astype(np.float32)
        hi = flat.astype(jnp.bfloat16)
        lo = (flat - hi.astype(np.float32)).astype(jnp.bfloat16)
        parts.append(np.concatenate([hi, hi, lo], axis=1))
    return np.stack(parts)


def broadcast_kernel(owner, depth, x_ref, o_ref, send_sem, recv_sem, whole_sem):
    del x_ref
    me = lax.axis_index("shot")
    z, y, c = me // 4, (me // 2) % 2, me % 2
    z0, y0, c0 = owner // 4, (owner // 2) % 2, owner % 2
    back = z0 + 1 if z0 < depth - 1 else z0 - 1
    count = o_ref.shape[1]
    is_owner = me == owner
    half = (c + c0) % 2
    main = (y + y0 + half) % 2 == 0
    root = (half == 1) & (z == z0) & (y == y0)
    extra = (half == 0) & (z == back) & (y != y0)
    up = main & (z >= z0) & (z < depth - 1)
    down = main & (z <= z0) & (z > 0)
    if back > z0:
        down = down | extra
    else:
        up = up | extra
    peer = me + 1 - 2 * c
    edges = [
        (0, up, me + 4),
        (1, down, me - 4),
        (2, (main & (z != z0)) | root, me + 2 - 4 * y),
        (3, jnp.logical_not(root), peer),
    ]

    def copy(at, send, arrive, target):
        return pltpu.make_async_remote_copy(
            src_ref=o_ref.at[at],
            dst_ref=o_ref.at[at],
            send_sem=send_sem.at[send],
            recv_sem=arrive,
            device_id={"shot": target},
            device_id_type=pl.DeviceIdType.MESH,
        )

    def forward(k):
        for slot, cond, target in edges:
            @pl.when(cond)
            def _():
                arrive = whole_sem if slot == 3 else recv_sem.at[k]
                copy((half, k), slot, arrive, target).start()

    def loop(body):
        def step(k, carry):
            body(k)
            return carry

        lax.fori_loop(0, count, step, 0)

    @pl.when(is_owner)
    def _():
        def step(k):
            copy((1, k), 4, recv_sem.at[k], peer).start()
            forward(k)

        loop(step)
        copy(1, 4, whole_sem, peer).wait_send()

    @pl.when(jnp.logical_not(is_owner))
    def _():
        def step(k):
            copy((half, k), 3, recv_sem.at[k], peer).wait_recv()
            forward(k)

        loop(step)
        copy(1 - half, 3, whole_sem, peer).wait_recv()

    for slot, cond, target in edges:
        @pl.when(cond)
        def _():
            copy(half, slot, whole_sem, target).wait_send()


def broadcast_rows(piece, owner, shots):
    shape = piece.shape
    count = shape[1] * shape[2] // PIECE_ROWS
    flat = piece.reshape(2, count, PIECE_ROWS, shape[3])

    def call(device):
        return pl.pallas_call(
            functools.partial(broadcast_kernel, device, shots // 4),
            out_shape=jax.ShapeDtypeStruct(flat.shape, flat.dtype),
            in_specs=[pl.BlockSpec(memory_space=pl.ANY)],
            out_specs=pl.BlockSpec(memory_space=pl.ANY),
            scratch_shapes=[
                pltpu.SemaphoreType.DMA((5,)),
                pltpu.SemaphoreType.DMA((count,)),
                pltpu.SemaphoreType.DMA,
            ],
            input_output_aliases={0: 0},
            compiler_params=pltpu.CompilerParams(has_side_effects=True),
            name="rows_from_%d" % device,
        )

    out = lax.switch(owner, [call(device) for device in range(shots)], flat)
    return out.reshape(shape)


def split(array):
    hi = array.astype(jnp.bfloat16)
    return hi, (array - hi.astype(jnp.float32)).astype(jnp.bfloat16)


def dot(left, right):
    return jnp.dot(left, right, preferred_element_type=jnp.float32)


def predict_kernel(
    own_ref, mine_ref, other_ref, row0_ref, row1_ref, table_ref, out_ref,
    left_hi, left_lo, freq_ref,
):
    nfreq = mine_ref.shape[1]
    rows = mine_ref.shape[2]
    tile = out_ref.shape[2]

    @pl.when(pl.program_id(0) == 0)
    def _():
        lane = lax.broadcasted_iota(jnp.int32, (rows, 2 * PANEL), 1)
        own = jnp.where(lane < PANEL, own_ref[0], own_ref[1]) == 1
        for f in range(nfreq):
            real = jnp.where(own, mine_ref[0, f], other_ref[0, f])
            imag = jnp.where(own, mine_ref[1, f], other_ref[1, f])
            cos, sin = middle(f)
            real, imag = real * cos - imag * sin, real * sin + imag * cos
            top = jnp.concatenate([real, -imag], axis=1)
            low = jnp.concatenate([imag, real], axis=1)
            hi, lo = split(jnp.concatenate([top, low], axis=0))
            left_hi[f] = hi
            left_lo[f] = lo

    for f in range(nfreq):
        right = jnp.concatenate(
            [row0_ref[0, f], row1_ref[0, f], row0_ref[1, f], row1_ref[1, f]], axis=0
        )
        hi, lo = split(right)
        both = dot(left_hi[f], hi) + dot(left_lo[f], hi) + dot(left_hi[f], lo)
        freq_ref[f] = both[:rows]
        freq_ref[nfreq + f] = both[rows:]

    half = SAMPLES // 2
    for g in range(rows // 8):
        at = slice(8 * g, 8 * g + 8)
        waves = []
        for i in (0, 1):
            part = freq_ref[i * nfreq : (i + 1) * nfreq, at, :].reshape(8 * nfreq, tile)
            hi, lo = split(part)
            waves.append(dot(table_ref[i], jnp.concatenate([hi, lo, hi], axis=0)))
        even, odd = waves
        out_ref[half:, at, :] = (even - odd).reshape(half, 8, tile)
        early = even + odd
        for j in range(half):
            out_ref[half - 1 - j, at, :] = early[8 * j : 8 * j + 8]


def predict(own, mine, other, row0, row1):
    _, nfreq, rows, width = mine.shape
    cols = row0.shape[3]
    tile = min(256, cols)
    big = jnp.asarray(kron_tables(nfreq))
    whole = pl.BlockSpec(mine.shape, lambda j: (0, 0, 0, 0))
    row_spec = pl.BlockSpec((2, nfreq, PANEL, tile), lambda j: (0, 0, 0, j))
    return pl.pallas_call(
        predict_kernel,
        grid=(cols // tile,),
        out_shape=jax.ShapeDtypeStruct((SAMPLES, rows, cols), jnp.float32),
        in_specs=[
            pl.BlockSpec(memory_space=pltpu.SMEM),
            whole,
            whole,
            row_spec,
            row_spec,
            pl.BlockSpec(big.shape, lambda j: (0, 0, 0)),
        ],
        out_specs=pl.BlockSpec((SAMPLES, rows, tile), lambda j: (0, 0, j)),
        scratch_shapes=[
            pltpu.VMEM((nfreq, 2 * rows, 4 * PANEL), jnp.bfloat16),
            pltpu.VMEM((nfreq, 2 * rows, 4 * PANEL), jnp.bfloat16),
            pltpu.VMEM((2 * nfreq, rows, tile), jnp.float32),
        ],
        compiler_params=pltpu.CompilerParams(vmem_limit_bytes=48 << 20),
        name="predict",
    )(own, mine, other, row0, row1, big)


def fetch_rows(source, start, shot_rows):
    length = min(shot_rows, PANEL)
    pieces = []
    for index_piece in range(PANEL // length):
        first = start + index_piece * length
        owner = first // shot_rows
        offset = first % shot_rows
        piece = lax.dynamic_slice_in_dim(source, offset, length, 2)
        pieces.append(from_root(piece, "shot", owner))
    return jnp.concatenate(pieces, axis=2)


def shards(tree, shots, recs, survey, panel_index):
    shot_rows = survey.shape[2]
    rec_cols = survey.shape[3]
    starts = [panel_index[step] * PANEL for step in range(STEPS)]
    columns = [
        lax.dynamic_slice_in_dim(survey, start % rec_cols, PANEL, 3) for start in starts
    ]
    owners = jnp.stack([start // rec_cols for start in starts])
    me = lax.axis_index("rec")
    mine = jnp.concatenate(columns, axis=3)
    if tree:
        other = lax.ppermute(mine, "rec", [(0, 1), (1, 0)])
        own = (owners == me).astype(jnp.int32)
        rows = []
        for start in starts:
            piece = lax.dynamic_slice_in_dim(survey, start % shot_rows, PANEL, 2)
            rows.append(broadcast_rows(piece, start // shot_rows, shots))
    else:
        wanted = jnp.repeat(owners == me, PANEL, total_repeat_length=STEPS * PANEL)
        mine = lax.psum(jnp.where(wanted, mine, 0.0), "rec")
        other = mine
        own = jnp.ones((STEPS,), jnp.int32)
        rows = [fetch_rows(survey, start, shot_rows) for start in starts]
    return predict(own, mine, other, rows[0], rows[1])


def solution(mesh):
    shots, recs = mesh.shape["shot"], mesh.shape["rec"]
    tree = (shots, recs) == (16, 2)
    return jax.shard_map(
        functools.partial(shards, tree, shots, recs),
        mesh=mesh,
        in_specs=(P(None, None, "shot", "rec"), P()),
        out_specs=P(None, "shot", "rec"),
        check_vma=False,
    )
```
